32 devices in a mesh: blk: 8 (over z, y), smp: 4 (over x, core).
Axes of the slice: x: 2, y: 2, z: 4, core: 2. Of those that a mesh axis runs over, the one named last changes fastest.
Arguments:
- forward_samples: bfloat16 [256, 65536], P('smp', 'blk'), may hold values from -0.375 to 0.375
- adjoint_samples: bfloat16 [256, 16384], P('smp', 'blk'), may hold values from -0.125 to 0.125
- probe_values: bfloat16 [16384, 192], P('blk'), may hold values from -6 to 6
- owners: int32 [16384, 1], P('blk'), may hold values from 0 to 7; in each aligned block of 2048 rows (0 to 2047, 2048 to 4095, ...) at most 512 rows name the same one
- block_ranks: int32 [8], P('blk'), may hold values from 64 to 256
- twiddle: float32 [2, 65536], P(None, 'blk'), may hold values from -1.2 to 1.2
Outputs:
- applied: bfloat16 [192, 65536], P('smp', 'blk')
The draws below stay inside these ranges and needn't reach their ends.
Inputs may be any that keep to these rules, and one draw needn't show every extreme that they name: `owners`: in the rows of one block index no owner block is named more than 512 times.
All inputs are finite; a program needn't handle non-finite values.
Results may differ from the reference program's by a relative error of at most 0.005.
Values may be sent and summed in bfloat16 or wider, within the bound.
A program may use at most 64 MiB of HBM per device.

```python
import math
import jax
import jax.numpy as jnp
import numpy as np
from jax import lax

SAMPLES = 256
BOX = 8192
VECTORS = 192
ADJ_ROWS = 2048
LEVELS = 2
BLOCKS = 8
CAPACITY = 512
N_BLK = 8


def with_ends(array, own_key, smallest, largest):
    spot = [jax.random.randint(jax.random.fold_in(own_key, axis), (), 0, length) for axis, length in enumerate(array.shape)]
    longest = array.shape.index(max(array.shape))
    beside = spot[:longest] + [(spot[longest] + 1) % array.shape[longest]] + spot[longest + 1:]
    return array.at[tuple(spot)].set(smallest).at[tuple(beside)].set(largest)


def block_levels(rng, shape, pieces, least, high):
    loudness, own = 1.0, jax.random.fold_in(rng, 6)
    for position, parts in pieces:
        steps = jnp.exp(jax.random.uniform(jax.random.fold_in(own, position), (parts,), jnp.float32, least / len(pieces), high / len(pieces)))
        loudness = loudness * jnp.repeat(steps, shape[position] // parts).reshape([-1 if axis == position else 1 for axis in range(len(shape))])
    return loudness


def shared_out(key, own, number, rows, amount, top, limit, lean):
    ranking = jax.random.permutation(key, amount)
    crowded, common = load_shares(amount, rows * top, limit, lean, True), load_shares(amount, rows * top, limit, lean, False)
    places = jnp.arange(amount)

    def named(lengths, rotation):
        used = int((lengths > 0).sum())
        fixed = max(1, used // 4)
        moved = fixed + (places - fixed + rotation * (used - fixed)) % max(1, amount - fixed)
        return jnp.zeros((amount,), jnp.int32).at[ranking[jnp.where(places < fixed, places, moved)]].set(jnp.asarray(lengths, jnp.int32))

    lengths = jnp.where(number % 4 == 0, named(crowded, number // 4), named(common, number - number // 4 - 1))
    mixed = jax.random.permutation(jax.random.fold_in(own, 3), amount)
    source_of, sink = mixed[0:amount // 2 * 2:2], mixed[1:amount // 2 * 2:2]
    margin = jnp.minimum(lengths[source_of] - 1, limit - lengths[sink]) // 2
    margin = jnp.where((source_of == ranking[0]) | (sink == ranking[0]) | (lengths[sink] == 0), 0, jnp.maximum(margin, 0))
    moved = jax.random.randint(jax.random.fold_in(own, 4), (amount // 2,), 0, 1 << 20) % (margin + 1)
    lengths = lengths.at[source_of].add(-moved).at[sink].add(moved)
    members = jnp.searchsorted(jnp.cumsum(lengths), jnp.arange(rows * top), side="right").astype(jnp.int32)
    listing = members.reshape(top, rows).T
    listing = listing[jax.random.permutation(jax.random.fold_in(own, 1), rows)]
    rotation = jax.random.randint(jax.random.fold_in(own, 2), (rows, 1), 0, top)
    return jnp.take_along_axis(listing, (jnp.arange(top)[None, :] + rotation) % top, axis=1)


def load_shares(amount, total, reach, lean, full):
    weights = [(1 << 20) // math.isqrt(grade ** lean) + 1 for grade in range(1, amount + 1)]
    largest = reach if full else min(reach, max(-(-total // amount), total * weights[0] // sum(weights)))
    least = 1 if total - largest >= amount - 1 else 0
    holding, spare = [largest] + [least] * (amount - 1), total - largest - least * (amount - 1)
    while spare > 0:
        movable = [i for i in range(1, amount) if holding[i] < largest] or [i for i in range(1, amount) if holding[i] < reach]
        mass, budget = sum([weights[i] for i in movable]), spare
        for i in movable:
            extra = min(reach - holding[i], max(1, budget * weights[i] // mass), spare)
            holding[i] = holding[i] + extra
            spare = spare - extra
    return np.array(holding)


def gaussian(key, shape, scale, reach, cuts=(), kind=jnp.bfloat16):
    values = jax.random.normal(key, shape, jnp.float32) * scale
    if len(cuts) > 0:
        values = block_levels(key, shape, cuts, -0.22, 0.18) * values
    return jnp.clip(values, min=-reach, max=reach).astype(kind)


def setup_inputs(seed: int = 0) -> dict:
    streams_of = jax.random.split(jax.random.key(seed), 7)
    forward_samples = gaussian(streams_of[0], (SAMPLES, BLOCKS * BOX), SAMPLES ** -0.5, 0.375, ((0, 4), (1, 8)))
    adjoint_samples = gaussian(streams_of[1], (SAMPLES, BLOCKS * ADJ_ROWS), ADJ_ROWS ** -0.5, 0.125, ((0, 4), (1, 8)))
    probe_values = gaussian(streams_of[2], (BLOCKS * ADJ_ROWS, VECTORS), 1.0, 6.0, ((0, 8),))
    owners_keys = jax.random.split(jax.random.fold_in(streams_of[3], 1), (BLOCKS * ADJ_ROWS) // ADJ_ROWS)
    owners_turns = jax.random.permutation(jax.random.fold_in(streams_of[3], 3), (BLOCKS * ADJ_ROWS) // ADJ_ROWS)
    owners = jax.vmap(lambda own, number: shared_out(jax.random.fold_in(streams_of[3], 2), own, number, ADJ_ROWS, BLOCKS, 1, CAPACITY, 2))(owners_keys, owners_turns).reshape((BLOCKS * ADJ_ROWS, 1))
    block_ranks = with_ends(jax.random.randint(streams_of[4], (BLOCKS,), SAMPLES // 4, SAMPLES + 1), jax.random.fold_in(streams_of[4], 1), SAMPLES // 4, SAMPLES).astype(jnp.int32)
    twiddle = jnp.clip(jax.random.uniform(streams_of[5], (LEVELS, BLOCKS * BOX), jnp.float32, -1.2, 1.2) * block_levels(streams_of[5], (LEVELS, BLOCKS * BOX), ((1, 8),), -0.4, 0.0), -1.2, 1.2)
    return dict(forward_samples=forward_samples, adjoint_samples=adjoint_samples, probe_values=probe_values, owners=owners, block_ranks=block_ranks, twiddle=twiddle)


def reference(forward_samples, adjoint_samples, probe_values, owners, block_ranks, twiddle):
    blocks = N_BLK
    owner_ids = owners[:, 0].astype(jnp.int32)
    per_block = ADJ_ROWS
    adj_rows = adjoint_samples.astype(jnp.float32).T.reshape(blocks, per_block, SAMPLES)
    probe_rows = probe_values.astype(jnp.float32).reshape(blocks, per_block, VECTORS)
    owner_rows = owner_ids.reshape(blocks, per_block)

    def accumulate(carry, items):
        adj_part, probe_part, owner_part = items
        outer = adj_part[:, :, None] * probe_part[:, None, :]
        return carry + jax.ops.segment_sum(outer, owner_part, num_segments=blocks), None

    start_sum = jnp.zeros((blocks, SAMPLES, VECTORS), jnp.float32)
    coeffs, unused = lax.scan(accumulate, start_sum, (adj_rows, probe_rows, owner_rows))
    keep_mask = (jnp.arange(SAMPLES, dtype=jnp.int32)[None, :] < block_ranks[:, None]).astype(jnp.float32)
    weights = lax.optimization_barrier((coeffs * keep_mask[:, :, None]).astype(jnp.bfloat16)).astype(jnp.float32)
    forward_grid = forward_samples.astype(jnp.float32).reshape(SAMPLES, blocks, BOX)
    field = jnp.einsum('bsv,sbm->vbm', weights, forward_grid)
    factors = twiddle.astype(jnp.float32).reshape(LEVELS, blocks, BOX)
    for level_index in range(LEVELS):
        distance = blocks // (2 ** (level_index + 1))
        partner_ids = jnp.bitwise_xor(jnp.arange(blocks, dtype=jnp.int32), distance)
        partner = jnp.take(field, partner_ids, axis=1)
        field = field + factors[level_index][None, :, :] * partner
    return field.reshape(VECTORS, blocks * BOX).astype(jnp.bfloat16)
```

```python
import functools

import jax
import jax.numpy as jnp
from jax import lax
from jax.experimental import pallas as pl
from jax.experimental.pallas import tpu as pltpu
from jax.sharding import PartitionSpec as P

DIRECT = 256
WIDTH = 128
EARLY = 2
MESH = pl.DeviceIdType.MESH


def kernel(
    blocks, smp, fwd, adj_in, probe_in, tw_in, owners_in, ranks, out,
    adj, probe, owners, mine, psend, precv, acr, acr_in, gath, left, limits,
    xa, fb, fs, fr, tw, oa, ob,
    load_sem, chain, p_send, p_recv, c_send, c_recv, g_send, g_recv, t_send, t_recv,
    xa_send, xa_recv, fb_send, fb_recv, f_send, f_recv, oa_send, oa_recv, ob_send, ob_recv,
    own_sem,
):
    levels = tw_in.shape[0]
    group = 2 ** levels
    low_count = blocks // group
    samples = fwd.shape[0]
    vectors = probe_in.shape[0]
    vlocal = vectors // smp
    wa = xa.shape[2]
    chunks, wc = fr.shape[0], fr.shape[3]
    wb = chunks * wc
    half = 2 * samples
    blk, j = lax.axis_index("blk"), lax.axis_index("smp")
    h, low = blk // low_count, blk % low_count
    q = h % 2
    inner = ((h + 1) // 2) % 2
    near, opp, diag = h + 1 - 2 * q, (h + 2) % group, group - 1 - h
    block_at = (h, near, opp, diag)
    rank = h * smp + j
    base = group * smp * wa

    def up(d):
        return (j + d) % smp

    def dev(hh, ll, jj):
        return {"blk": hh * low_count + ll, "smp": jj}

    def aligned(start, size):
        return pl.ds(pl.multiple_of(start, size), size)

    def remote(src, dst, send, recv, where):
        return pltpu.make_async_remote_copy(
            src_ref=src, dst_ref=dst, send_sem=send, recv_sem=recv,
            device_id=where, device_id_type=MESH,
        )

    def each(first, last, step):
        if last - first > 2:
            lax.fori_loop(first, last, lambda d, c: (step(d), c)[1], 0)
        else:
            for d in range(first, last):
                step(d)

    loads = [
        pltpu.make_async_copy(src, dst, load_sem.at[i])
        for i, (src, dst) in enumerate(((owners_in, owners), (adj_in, adj), (probe_in, probe)))
    ]
    for c in loads:
        c.start()

    barrier = pltpu.get_barrier_semaphore()

    def signal(sem, where):
        pl.semaphore_signal(sem, inc=1, device_id=where, device_id_type=MESH)

    def greet(hh):
        for dj in range(smp):
            signal(barrier, dev(hh, low, up(dj)))

    below, above = h > 0, h < group - 1
    sides = jnp.where(below, 1, 0) + jnp.where(above, 1, 0)
    pl.when(above)(lambda: greet(h + 1))
    pl.when(below)(lambda: greet(h - 1))
    for dj in range(1, smp):
        signal(barrier, dev(h, low, up(dj)))

    def greet_low(d):
        lo = (low + d) % low_count
        signal(barrier, dev(h, lo, j))
        signal(barrier, dev(near, lo, j))

    each(1, low_count, greet_low)

    def pass_on(sem):
        pl.when(above)(lambda: signal(sem, dev(h + 1, low, j)))
        pl.when(below)(lambda: signal(sem, dev(h - 1, low, j)))

    def fa_copy(x, hh, dj):
        to = hh * smp + up(dj)
        slot = x * smp + dj
        return remote(
            fwd.at[:, aligned(to * wa, wa)], xa.at[h, aligned(j * samples, samples), :],
            xa_send.at[slot], xa_recv.at[slot], dev(hh, low, up(dj)),
        )

    first_x, second_x = 1 + 2 * inner, 3 - 2 * inner
    first_h = inner * diag + (1 - inner) * near
    second_h = inner * near + (1 - inner) * diag
    fa = {
        "first": [fa_copy(first_x, first_h, dj) for dj in range(smp)],
        "opp": [fa_copy(2, opp, dj) for dj in range(smp)],
        "second": [fa_copy(second_x, second_h, dj) for dj in range(smp)],
        "own": [fa_copy(0, h, dj) for dj in range(1, smp)],
    }

    def fb_copy(d):
        return remote(
            fwd.at[:, aligned(base + up(d) * group * wb, group * wb)],
            fb.at[aligned(j * samples, samples), :],
            fb_send.at[d], fb_recv.at[d], dev(h, low, up(d)),
        )

    fb_copies = [fb_copy(d) for d in range(1, smp)]
    owned = [
        pltpu.make_async_copy(
            fwd.at[:, aligned(rank * wa, wa)], xa.at[h, aligned(j * samples, samples), :],
            own_sem.at[0],
        ),
        pltpu.make_async_copy(
            fwd.at[:, aligned(base + j * group * wb, group * wb)],
            fb.at[aligned(j * samples, samples), :], own_sem.at[1],
        ),
    ]

    pl.semaphore_wait(barrier, smp * sides + smp - 1 + 2 * (low_count - 1))
    pass_on(chain.at[0])

    def begin(copies):
        for c in copies:
            c.start()

    pl.when(inner == 1)(lambda: begin(fa["first"]))
    for c in loads:
        c.wait()

    def partial_sums(lo):
        stacked = jnp.concatenate(
            [
                adj[...] * (owners[...] == hh * low_count + lo).astype(jnp.bfloat16)
                for side in range(2)
                for hh in range(side, group, 2)
            ],
            axis=0,
        )
        return lax.dot_general(
            probe[...], stacked, (((1,), (1,)), ((), ())), preferred_element_type=jnp.float32
        )

    def part_copy(d, side):
        where = dev((h, near)[side], (low + d) % low_count, j)
        mark = q if side == 0 else 1 - q
        return remote(
            psend.at[d, mark], precv.at[d, side], p_send.at[d, side], p_recv.at[d, side], where
        )

    def send_parts(d):
        total = partial_sums((low + d) % low_count)
        for side in range(2):
            psend[d, side] = total[:, side * half : (side + 1) * half].astype(jnp.bfloat16)
        part_copy(d, 0).start()
        part_copy(d, 1).start()

    each(1, low_count, send_parts)
    total = partial_sums(low)
    for side in range(2):
        piece = total[:, side * half : (side + 1) * half]
        mine[side] = piece
        psend[0, side] = piece.astype(jnp.bfloat16)
    part_copy(0, 1).start()
    limits[0] = jnp.full(limits.shape[1:], ranks[0].astype(jnp.float32))

    pl.semaphore_wait(chain.at[0], sides)
    pass_on(chain.at[1])
    limit_copy = remote(
        limits.at[0], limits.at[1], t_send.at[0, 0], t_recv.at[0, 0], dev(opp, low, j)
    )
    limit_copy.start()

    @pl.when(inner == 1)
    def _():
        begin(fa["opp"][:EARLY])
        begin(fa["second"])

    pl.when(inner == 0)(lambda: begin(fa["first"]))
    begin(owned)
    begin(fb_copies)

    small = []
    for x in range(group):
        hh = block_at[x]
        for i, (start, size, at) in enumerate((
            ((hh * smp + j) * wa, wa, 0), (base + (j * group + hh) * wb, wb, wa),
        )):
            src, dst = tw_in.at[:, aligned(start, size)], tw.at[h, :, at : at + size]
            if x == 0:
                small.append(pltpu.make_async_copy(src, dst, own_sem.at[2 + i]))
            else:
                small.append(
                    remote(src, dst, t_send.at[x, i], t_recv.at[x, i], dev(hh, low, j))
                )
    part_copy(0, 1).wait()
    mine[q] += precv[0, 1].astype(jnp.float32)

    def add_parts(d):
        for side in range(2):
            part_copy(d, side).wait()
        mine[q] += precv[d, 0].astype(jnp.float32) + precv[d, 1].astype(jnp.float32)

    each(1, low_count, add_parts)
    acr[...] = mine[q].astype(jnp.bfloat16)
    acr_copy = remote(acr, acr_in, c_send, c_recv, dev(opp, low, j))
    acr_copy.start()
    pl.when(inner == 1)(lambda: begin(fa["opp"][EARLY:]))
    pl.semaphore_wait(chain.at[1], sides)
    limit_copy.wait()

    lane = lax.broadcasted_iota(jnp.int32, (1, half), 1)
    number = (j * samples + lane % samples).astype(jnp.float32)
    limit = jnp.where(
        lane // samples == h // 2, limits[0, 0:1, 0:1], limits[1, 0:1, 0:1]
    )
    keep = (number < limit).astype(jnp.float32)
    acr_copy.wait()
    gath[q, j] = ((mine[q] + acr_in[...].astype(jnp.float32)) * keep).astype(jnp.bfloat16)

    def gath_copy(x, dj):
        return remote(
            gath.at[q, j], gath.at[q, j], g_send.at[x, dj], g_recv.at[x, dj],
            dev(block_at[x], low, up(dj)),
        )

    same = [gath_copy(0, dj) for dj in range(1, smp)]
    cross = [gath_copy(1, dj) for dj in range(smp)]
    begin(same)

    @pl.when(inner == 0)
    def _():
        begin(fa["opp"])
        begin(fa["second"])

    begin(cross)
    begin(fa["own"])
    begin(small)

    def build(side):
        front = lane < samples
        for jj in range(0, smp, 2):
            a = gath[side, jj].astype(jnp.float32)
            b = gath[side, jj + 1].astype(jnp.float32)
            cols = slice(jj * samples, (jj + 2) * samples)
            left[side, :, cols] = jnp.where(front, a, pltpu.roll(b, samples, 1)).astype(
                jnp.bfloat16
            )
            left[side + 2, :, cols] = jnp.where(front, pltpu.roll(a, samples, 1), b).astype(
                jnp.bfloat16
            )

    for c in owned + fb_copies + same:
        c.wait()
    build(q)

    f_copies = {}
    for k in range(chunks):
        for x in (2, 3, 1, 0):
            hh = block_at[x]
            product = jnp.dot(
                left[h], fb[:, aligned(hh * wb + k * wc, wc)], preferred_element_type=jnp.float32
            ).astype(jnp.bfloat16)
            if x == 0:
                fr[k, h] = product
                continue
            fs[k, x] = product
            f_copies[k, x] = remote(
                fs.at[k, x], fr.at[k, h], f_send.at[k, x], f_recv.at[k, x], dev(hh, low, j)
            )
            f_copies[k, x].start()

    def butterfly(field, at):
        for level in range(levels):
            distance = group >> (level + 1)
            field = [
                field[hh] + tw[hh, level : level + 1, at : at + wc] * field[hh ^ distance]
                for hh in range(group)
            ]
        return field

    sent = []

    def send_out(src, cols, send, recv, spare):
        for x in (2, 3, 1, 0):
            for dj in range(smp):
                piece = src.at[block_at[x], aligned(up(dj) * vlocal, vlocal), :]
                dst = out.at[:, cols]
                if (x, dj) == (0, 0):
                    c = pltpu.make_async_copy(piece, dst, spare)
                else:
                    slot = x * smp + dj
                    c = remote(
                        piece, dst, send.at[slot], recv.at[slot], dev(block_at[x], low, up(dj))
                    )
                c.start()
                sent.append(c)

    for c in cross:
        c.wait()
    build(1 - q)
    for name in fa:
        for c in fa[name]:
            c.wait()
    for c in small:
        c.wait()
    for at in range(0, wa, wc):
        field = [
            jnp.dot(left[hh], xa[hh, :, at : at + wc], preferred_element_type=jnp.float32)
            for hh in range(group)
        ]
        field = butterfly(field, at)
        for hh in range(group):
            oa[hh, :, at : at + wc] = field[hh].astype(jnp.bfloat16)
    send_out(oa, aligned(rank * wa, wa), oa_send, oa_recv, own_sem.at[4])
    for k in range(chunks):
        for x in (1, 2, 3):
            f_copies[k, x].wait()
        field = butterfly([fr[k, hh].astype(jnp.float32) for hh in range(group)], wa + k * wc)
        for hh in range(group):
            ob[k, hh] = field[hh].astype(jnp.bfloat16)
        cols = aligned(base + (j * group + h) * wb + k * wc, wc)
        send_out(ob.at[k], cols, ob_send.at[k], ob_recv.at[k], own_sem.at[5 + k])
    for c in sent:
        c.wait()


def body(blocks, smp, fwd, adj, probe, owners, ranks, twiddle):
    samples, box = fwd.shape
    rows, vectors = probe.shape
    levels = twiddle.shape[0]
    group = 2 ** levels
    low_count = blocks // group
    peers = group * smp
    span = box // peers
    wa, wc = DIRECT, WIDTH
    wb = span - wa
    chunks = wb // wc
    half = 2 * samples
    bf16, f32 = jnp.bfloat16, jnp.float32
    dma = pltpu.SemaphoreType.DMA
    hbm = pl.BlockSpec(memory_space=pltpu.HBM)
    result = 2 * (vectors // smp) * box
    return pl.pallas_call(
        functools.partial(kernel, blocks, smp),
        out_shape=pltpu.VMEM((vectors // smp, box), bf16),
        in_specs=[
            hbm, hbm, hbm, hbm, hbm,
            pl.BlockSpec(memory_space=pltpu.SMEM),
        ],
        out_specs=pl.BlockSpec(memory_space=pltpu.VMEM),
        scratch_shapes=[
            pltpu.VMEM(adj.shape, bf16),
            pltpu.VMEM((vectors, rows), bf16),
            pltpu.VMEM((1, rows), jnp.int32),
            pltpu.VMEM((2, vectors, half), f32),
            pltpu.VMEM((low_count, 2, vectors, half), bf16),
            pltpu.VMEM((low_count, 2, vectors, half), bf16),
            pltpu.VMEM((vectors, half), bf16),
            pltpu.VMEM((vectors, half), bf16),
            pltpu.VMEM((2, smp, vectors, half), bf16),
            pltpu.VMEM((group, vectors, smp * samples), bf16),
            pltpu.VMEM((2, 8, 128), f32),
            pltpu.VMEM((group, smp * samples, wa), bf16),
            pltpu.VMEM((smp * samples, group * wb), bf16),
            pltpu.VMEM((chunks, group, vectors, wc), bf16),
            pltpu.VMEM((chunks, group, vectors, wc), bf16),
            pltpu.VMEM((group, levels, span), f32),
            pltpu.VMEM((group, vectors, wa), bf16),
            pltpu.VMEM((chunks, group, vectors, wc), bf16),
            dma((3,)), pltpu.SemaphoreType.REGULAR((2,)),
            dma((low_count, 2)), dma((low_count, 2)),
            dma, dma,
            dma((2, smp)), dma((2, smp)),
            dma((group, 2)), dma((group, 2)),
            dma((peers,)), dma((peers,)),
            dma((smp,)), dma((smp,)),
            dma((chunks, group)), dma((chunks, group)),
            dma((peers,)), dma((peers,)),
            dma((chunks, peers)), dma((chunks, peers)),
            dma((5 + chunks,)),
        ],
        compiler_params=pltpu.CompilerParams(
            collective_id=0, has_side_effects=True, vmem_limit_bytes=67_030_000 - result
        ),
        name="butterfly",
    )(fwd, adj, probe.T, twiddle, owners.reshape(1, rows), ranks)


def solution(mesh):
    in_specs = (
        P("smp", "blk"),
        P("smp", "blk"),
        P("blk", None),
        P("blk", None),
        P("blk"),
        P(None, "blk"),
    )
    return jax.shard_map(
        functools.partial(body, mesh.shape["blk"], mesh.shape["smp"]),
        mesh=mesh, in_specs=in_specs, out_specs=P("smp", "blk"), check_vma=False,
    )
```
